512 devices in a mesh: fsdp: 64 (over x, z, y_hi), dp: 8 (over y_lo, core).
Axes of the slice: x: 4, y: 8 (y_hi: 2, y_lo: 4; y = y_hi * 4 + y_lo), z: 8, core: 2. Of those that a mesh axis runs over, the one named last changes fastest.
Arguments:
- tokens: bfloat16 [65536, 8192], P(('fsdp', 'dp')), may hold values from -6 to 6
- token_adapter_index: int32 [65536, 1], P(('fsdp', 'dp')), may hold values from 0 to 63; in each aligned block of 128 rows (0 to 127, 128 to 255, ...) at most 3 rows name the same one
- adapter_storage_index: int32 [64], replicated, may hold values from 0 to 63, each once
- frozen_value_weight: bfloat16 [8192, 512], P(('fsdp', 'dp')), may hold values from -0.0625 to 0.0625
- frozen_value_bias: bfloat16 [512], replicated, may hold values from -3 to 3
- adapter_down_weight: bfloat16 [64, 8192, 64], P('fsdp'), may hold values from -0.0625 to 0.0625
- adapter_up_weight: bfloat16 [64, 64, 512], P('fsdp'), may hold values from -0.75 to 0.75
- cotangent: bfloat16 [65536, 512], P(('fsdp', 'dp')), may hold values from -0.1875 to 0.1875
Outputs:
- values: bfloat16 [65536, 512], P(('fsdp', 'dp'))
- grad_down: float32 [64, 8192, 64], P('fsdp', 'dp')
- grad_up: float32 [64, 64, 512], P('fsdp', None, 'dp')
The draws below stay inside these ranges and needn't reach their ends.
Inputs may be any that keep to these rules, and one draw needn't show every extreme that they name: `token_adapter_index`: within the 128 rows of one device no adapter is named by more than 3 rows. `adapter_storage_index`: each storage index appears once.
All inputs are finite; a program needn't handle non-finite values.
Results may differ from the reference program's by a relative error of at most 0.0048.
Values may be sent and summed in bfloat16 or wider, within the bound.
No kernel may reach another device: no remote copies, remote signals or barrier semaphores. Data moves between devices by JAX's collectives and lax.ppermute only.
A program may use at most 64 MiB of HBM per device.

```python
import math
import jax
import jax.numpy as jnp
import numpy as np
from jax import lax

MODEL_DIM = 8192
VALUE_OUT_WIDTH = 512
ADAPTER_RANK = 64
TOK_DEV = 128
TOKENS = 65536
ADAPTER_COUNT = 64
CAP = 3
N_FSDP = 64
N_DP = 8


def levels(own_key, shape, shards, smallest, high):
    gain = 1.0
    for position, parts in shards:
        steps = jax.random.uniform(jax.random.fold_in(jax.random.fold_in(own_key, 6), position), (parts,), jnp.float32, smallest / len(shards), high / len(shards))
        gain = gain * jnp.repeat(jnp.exp(steps), shape[position] // parts).reshape((-1,) + (1,) * (len(shape) - 1 - position))
    return gain


def deal_out(own_key, own, number, rows, number_of, top, limit, skew):
    ranking = jax.random.permutation(own_key, number_of)
    crowded, common = shares(number_of, rows * top, limit, skew, True), shares(number_of, rows * top, limit, skew, False)
    places = jnp.arange(number_of)

    def named(lengths, rotation):
        used = int((lengths > 0).sum())
        fixed = max(1, used // 4)
        moved = fixed + (places - fixed + rotation * (used - fixed)) % max(1, number_of - fixed)
        return jnp.zeros((number_of,), jnp.int32).at[ranking[jnp.where(places < fixed, places, moved)]].set(jnp.asarray(lengths, jnp.int32))

    lengths = jnp.where(number % 4 == 0, named(crowded, number // 4), named(common, number - number // 4 - 1))
    mixed = jax.random.permutation(jax.random.fold_in(own, 3), number_of)
    source_of, sink = mixed[0:number_of // 2 * 2:2], mixed[1:number_of // 2 * 2:2]
    margin = jnp.minimum(lengths[source_of] - 1, limit - lengths[sink]) // 2
    margin = jnp.where((source_of == ranking[0]) | (sink == ranking[0]) | (lengths[sink] == 0), 0, jnp.maximum(margin, 0))
    moved = jax.random.randint(jax.random.fold_in(own, 4), (number_of // 2,), 0, 1 << 20) % (margin + 1)
    lengths = lengths.at[source_of].add(-moved).at[sink].add(moved)
    labels = jnp.searchsorted(jnp.cumsum(lengths), jnp.arange(rows * top), side="right").astype(jnp.int32)
    table = labels.reshape(top, rows).T
    table = table[jax.random.permutation(jax.random.fold_in(own, 1), rows)]
    rotation = jax.random.randint(jax.random.fold_in(own, 2), (rows, 1), 0, top)
    return jnp.take_along_axis(table, (jnp.arange(top)[None, :] + rotation) % top, axis=1)


def shares(amount, total, limit, skew, full):
    weights = [(1 << 20) // math.isqrt(standing ** skew) + 1 for standing in range(1, amount + 1)]
    largest = limit if full else min(limit, max(-(-total // amount), total * weights[0] // sum(weights)))
    least = 1 if total - largest >= amount - 1 else 0
    given, spare = [largest] + [least] * (amount - 1), total - largest - least * (amount - 1)
    while spare > 0:
        movable = [i for i in range(1, amount) if given[i] < largest] or [i for i in range(1, amount) if given[i] < limit]
        mass, left = sum([weights[i] for i in movable]), spare
        for i in movable:
            extra = min(limit - given[i], max(1, left * weights[i] // mass), spare)
            given[i] = given[i] + extra
            spare = spare - extra
    return np.array(given)


def noise(key, extent, spread, reach, pieces=(), held_as=jnp.bfloat16):
    entries = jax.random.normal(key, extent, jnp.float32) * spread
    if len(pieces) > 0:
        entries = levels(key, extent, pieces, -0.22, 0.18) * entries
    return jnp.clip(entries, min=-reach, max=reach).astype(held_as)


def setup_inputs(seed: int = 0) -> dict:
    seeds = jax.random.split(jax.random.key(seed), 9)
    tokens = noise(seeds[0], (TOKENS, MODEL_DIM), 1.0, 6.0, ((0, 512),))
    token_adapter_index_keys = jax.random.split(jax.random.fold_in(seeds[1], 1), TOKENS // TOK_DEV)
    token_adapter_index_turns = jax.random.permutation(jax.random.fold_in(seeds[1], 3), TOKENS // TOK_DEV)
    token_adapter_index = jax.vmap(lambda own, number: deal_out(jax.random.fold_in(seeds[1], 2), own, number, TOK_DEV, ADAPTER_COUNT, 1, CAP, 2))(token_adapter_index_keys, token_adapter_index_turns).reshape((TOKENS, 1))
    adapter_storage_index = jax.random.permutation(seeds[2], ADAPTER_COUNT).astype(jnp.int32)
    frozen_value_weight = noise(seeds[3], (MODEL_DIM, VALUE_OUT_WIDTH), MODEL_DIM ** -0.5, 0.0625, ((0, 512),))
    frozen_value_bias = noise(seeds[4], (VALUE_OUT_WIDTH,), 0.5, 3.0)
    adapter_down_weight = noise(seeds[5], (ADAPTER_COUNT, MODEL_DIM, ADAPTER_RANK), MODEL_DIM ** -0.5, 0.0625, ((0, 64),))
    adapter_up_weight = noise(seeds[6], (ADAPTER_COUNT, ADAPTER_RANK, VALUE_OUT_WIDTH), ADAPTER_RANK ** -0.5, 0.75, ((0, 64),))
    cotangent = noise(seeds[7], (TOKENS, VALUE_OUT_WIDTH), 0.03125, 0.1875, ((0, 512),))
    return dict(tokens=tokens, token_adapter_index=token_adapter_index, adapter_storage_index=adapter_storage_index, frozen_value_weight=frozen_value_weight, frozen_value_bias=frozen_value_bias, adapter_down_weight=adapter_down_weight, adapter_up_weight=adapter_up_weight, cotangent=cotangent)


def reference(tokens, token_adapter_index, adapter_storage_index, frozen_value_weight, frozen_value_bias, adapter_down_weight, adapter_up_weight, cotangent):
    owner_index = jnp.take(adapter_storage_index, token_adapter_index[:, 0]).astype(jnp.int32)
    onehot = (owner_index[:, None] == jnp.arange(ADAPTER_COUNT, dtype=jnp.int32)[None, :]).astype(jnp.int32)
    place = jnp.sum((jnp.cumsum(onehot, 0).astype(jnp.int32) - onehot) * onehot, 1).astype(jnp.int32)
    longest = CAP * N_FSDP * N_DP
    index_table = jnp.full((ADAPTER_COUNT, longest), TOKENS, jnp.int32)
    index_table = index_table.at[owner_index, place].set(jnp.arange(TOKENS, dtype=jnp.int32))
    token_pad = jnp.concatenate([tokens, jnp.zeros((1, MODEL_DIM), tokens.dtype)], 0)
    cot_pad = jnp.concatenate([cotangent, jnp.zeros((1, VALUE_OUT_WIDTH), cotangent.dtype)], 0)

    def per_adapter(adapter_number):
        picks = index_table[adapter_number]
        token_input_rows = token_pad[picks]
        cotangent_rows = cot_pad[picks]
        rank_activation = jnp.dot(token_input_rows, adapter_down_weight[adapter_number], preferred_element_type=jnp.float32).astype(jnp.bfloat16)
        adapter_delta = jnp.dot(rank_activation, adapter_up_weight[adapter_number], preferred_element_type=jnp.float32).astype(jnp.bfloat16)
        rank_cotangent = jnp.dot(cotangent_rows, adapter_up_weight[adapter_number].T, preferred_element_type=jnp.float32).astype(jnp.bfloat16)
        grad_down = jnp.dot(token_input_rows.T, rank_cotangent, preferred_element_type=jnp.float32)
        grad_up = jnp.dot(rank_activation.T, cotangent_rows, preferred_element_type=jnp.float32)
        return adapter_delta, grad_down, grad_up

    corrections, grad_down, grad_up = lax.map(per_adapter, jnp.arange(ADAPTER_COUNT, dtype=jnp.int32))
    placed = jnp.zeros((TOKENS + 1, VALUE_OUT_WIDTH), corrections.dtype)
    placed = placed.at[index_table.reshape(-1)].set(corrections.reshape(-1, VALUE_OUT_WIDTH))[:TOKENS]
    base_value = jnp.dot(tokens, frozen_value_weight, preferred_element_type=jnp.float32) + frozen_value_bias.astype(jnp.float32)
    values = (base_value + placed.astype(jnp.float32)).astype(jnp.bfloat16)
    return values, grad_down, grad_up
```

```python
import jax
import jax.numpy as jnp
from jax import lax
from jax.experimental import pallas as pl
from jax.experimental.pallas import tpu as pltpu
from jax.sharding import PartitionSpec as P

SLOTS = 3
Q = 8
F32 = jnp.float32
BF16 = jnp.bfloat16


def iota(shape, dimension):
    return lax.broadcasted_iota(jnp.int32, shape, dimension)


def nn(a, b):
    return lax.dot_general(a, b, (((1,), (0,)), ((), ())), preferred_element_type=F32)


def nt(a, b):
    return lax.dot_general(a, b, (((1,), (1,)), ((), ())), preferred_element_type=F32)


def tn(a, b):
    return lax.dot_general(a, b, (((0,), (0,)), ((), ())), preferred_element_type=F32)


def dispatch_kernel(storage_ref, index_ref, tokens_ref, cot_ref, sent_ref, place_ref, pick_ref):
    count, width = tokens_ref.shape
    rows = sent_ref.shape[0]
    chunk = width // Q
    half = cot_ref.shape[1] // 2
    index = index_ref[...]
    owner = jnp.zeros_like(index)
    for n in range(rows // Q):
        owner = jnp.where(index == n, storage_ref[n], owner)
    row = iota((rows, count), 0)
    q = row % Q
    mine = (row // Q) == jnp.broadcast_to(owner, (rows, count))
    mine_f = jnp.where(mine, 1.0, 0.0).astype(F32)
    earlier = jnp.where(iota((count, count), 0) < iota((count, count), 1), 1.0, 0.0).astype(BF16)
    rank = nn(mine_f.astype(BF16), earlier).astype(jnp.int32)
    for s in range(SLOTS):
        here = mine & (rank == s)
        for i in range(Q):
            pick_ref[s, :, i * count : (i + 1) * count] = jnp.where(
                here & (q == i), 1.0, 0.0
            ).astype(BF16)
    for h in range(2):
        both = mine & (rank == q // 2) & (q % 2 == h)
        place_ref[h] = jnp.where(both, 1.0, 0.0).astype(BF16)
        sent = nn(place_ref[h], cot_ref[:, h * half : (h + 1) * half])
        if h == 0:
            total = sent
        else:
            total = total + sent
    sent_ref[:, SLOTS * chunk :] = total.astype(BF16)
    step = 256

    @pl.loop(0, chunk // step)
    def _(block):
        start = block * step
        piece = jnp.concatenate(
            [
                tokens_ref[:, pl.ds(pl.multiple_of(i * chunk + start, step), step)]
                for i in range(Q)
            ],
            axis=0,
        )
        for s in range(SLOTS):
            sent_ref[:, pl.ds(pl.multiple_of(s * chunk + start, step), step)] = nn(
                pick_ref[s], piece
            ).astype(BF16)


def fold(masked, rank):
    rows, wide = masked.shape
    total = masked[:, : 2 * rank]
    for k in range(1, wide // (2 * rank)):
        total = total + masked[:, 2 * rank * k : 2 * rank * (k + 1)]
    total = total + pltpu.roll(total, rank, 1)
    total = jnp.sum(total.reshape(rows // Q, Q, 2 * rank), axis=1, keepdims=True)
    return jnp.broadcast_to(total, (rows // Q, Q, 2 * rank)).reshape(rows, 2 * rank)


def stacked_up(up_ref):
    half = up_ref.shape[1] // 2
    return jnp.concatenate([up_ref[:, :half], up_ref[:, half:]], axis=0)


def correct_kernel(arrived_ref, down_ref, up_ref, back_ref, low_ref):
    rows = arrived_ref.shape[0]
    rank, width = down_ref.shape
    chunk = width // Q
    q = iota((rows, 2 * rank), 0) % Q
    part = iota((rows, 2 * rank), 1) // rank
    wide_q = iota((rows, Q * rank), 0) % Q == iota((rows, Q * rank), 1) // rank
    down = jnp.concatenate([down_ref[:, i * chunk : (i + 1) * chunk] for i in range(Q)], axis=0)
    low = jnp.zeros((rows, 2 * rank), F32)
    for s in range(SLOTS):
        full = nt(arrived_ref[:, s * chunk : (s + 1) * chunk], down)
        low = jnp.where(q // 2 == s, fold(jnp.where(wide_q, full, 0.0), rank), low)
    low = jnp.where(part == q % 2, low, 0.0).astype(BF16)
    low_ref[...] = low
    back_ref[...] = nn(low, stacked_up(up_ref)).astype(BF16)


def grads_kernel(arrived_ref, up_ref, low_ref, grad_ref):
    rows = arrived_ref.shape[0]
    rank = up_ref.shape[0]
    chunk = grad_ref.shape[1] - 2 * rank
    cot = arrived_ref[:, SLOTS * chunk :]
    q = iota((rows, 2 * rank), 0) % Q
    part = iota((rows, 2 * rank), 1) // rank
    wide_q = iota((rows, Q * rank), 0) % Q == iota((rows, Q * rank), 1) // rank
    both = nt(cot, stacked_up(up_ref))
    lefts = []
    for s in range(SLOTS):
        back = fold(jnp.where((q // 2 == s) & (part == q % 2), both, 0.0), rank)
        lefts.append(
            jnp.where(wide_q, jnp.concatenate([back] * (Q // 2), axis=1), 0.0).astype(BF16)
        )
    left = jnp.concatenate(lefts, axis=0)
    step = 256
    for start in range(0, chunk, step):
        right = jnp.concatenate(
            [
                arrived_ref[:, s * chunk + start : s * chunk + start + step]
                for s in range(SLOTS)
            ],
            axis=0,
        )
        grad_ref[:, start : start + step] = tn(left, right).astype(BF16)
    up = tn(low_ref[...], cot).astype(BF16)
    per_half = Q // 2
    for d in range(Q):
        column = (d % per_half) // 2 * 2 * rank
        first = d // per_half * rank
        grad_ref[d * rank : (d + 1) * rank, chunk:] = up[
            first : first + rank, column : column + 2 * rank
        ]


def place_kernel(base0_ref, base1_ref, place_ref, back_ref, values_ref):
    half = back_ref.shape[1]
    for h, base_ref in enumerate((base0_ref, base1_ref)):
        placed = tn(place_ref[h], back_ref[...])
        values_ref[:, h * half : (h + 1) * half] = (base_ref[...] + placed).astype(BF16)


def vmem(number):
    return [pl.BlockSpec(memory_space=pltpu.VMEM)] * number


PARAMS = pltpu.CompilerParams(vmem_limit_bytes=48 << 20)


def body(
    tokens,
    token_adapter_index,
    adapter_storage_index,
    frozen_value_weight,
    frozen_value_bias,
    adapter_down_weight,
    adapter_up_weight,
    cotangent,
):
    count, width = tokens.shape
    out_width = frozen_value_weight.shape[1]
    fsdp = lax.axis_size("fsdp")
    dp = lax.axis_size("dp")
    rank = adapter_up_weight.shape[1]
    half = out_width // 2
    chunk = width // Q
    rows = fsdp * Q
    columns = SLOTS * chunk + half

    weights = []
    for h in range(2):
        weights.append(
            lax.all_gather(
                frozen_value_weight[:, h * half : (h + 1) * half],
                ("fsdp", "dp"),
                axis=0,
                tiled=True,
            )
        )
    sent, place = pl.pallas_call(
        dispatch_kernel,
        out_shape=(
            jax.ShapeDtypeStruct((rows, columns), BF16),
            jax.ShapeDtypeStruct((2, rows, count), BF16),
        ),
        in_specs=[pl.BlockSpec(memory_space=pltpu.SMEM)] + vmem(3),
        out_specs=tuple(vmem(2)),
        scratch_shapes=[pltpu.VMEM((SLOTS, rows, Q * count), BF16)],
        compiler_params=PARAMS,
        name="dispatch",
    )(adapter_storage_index, token_adapter_index.reshape(1, count), tokens, cotangent)
    arrived = lax.all_to_all(
        sent.reshape(fsdp, Q, columns), "fsdp", split_axis=0, concat_axis=0, tiled=True
    ).reshape(rows, columns)
    down = jnp.swapaxes(adapter_down_weight[0], 0, 1)
    up = adapter_up_weight[0]
    back, low = pl.pallas_call(
        correct_kernel,
        out_shape=(
            jax.ShapeDtypeStruct((rows, half), BF16),
            jax.ShapeDtypeStruct((rows, 2 * rank), BF16),
        ),
        in_specs=vmem(3),
        out_specs=tuple(vmem(2)),
        compiler_params=PARAMS,
        name="correct",
    )(arrived, down, up)
    back = lax.all_to_all(
        back.reshape(fsdp, Q, half), "fsdp", split_axis=0, concat_axis=0, tiled=True
    ).reshape(rows, half)
    grads = pl.pallas_call(
        grads_kernel,
        out_shape=jax.ShapeDtypeStruct((dp * rank, chunk + 2 * rank), BF16),
        in_specs=vmem(3),
        out_specs=vmem(1)[0],
        compiler_params=PARAMS,
        name="grads",
    )(arrived, up, low)
    grads = lax.all_to_all(
        grads.reshape(dp, rank, chunk + 2 * rank),
        "dp",
        split_axis=0,
        concat_axis=0,
        tiled=True,
    )
    grads = jnp.sum(grads.astype(F32), axis=0)
    odd = lax.axis_index("dp") % 2 == 1
    grad_up = jnp.where(odd, grads[:, chunk + rank :], grads[:, chunk : chunk + rank])
    grad_down = jnp.swapaxes(grads[:, :chunk], 0, 1)
    base = [
        jnp.dot(tokens, weights[h], preferred_element_type=F32)
        + frozen_value_bias[h * half : (h + 1) * half].astype(F32)
        for h in range(2)
    ]
    values = pl.pallas_call(
        place_kernel,
        out_shape=jax.ShapeDtypeStruct((count, out_width), BF16),
        in_specs=vmem(4),
        out_specs=vmem(1)[0],
        compiler_params=PARAMS,
        name="place",
    )(*base, place, back)
    return values, grad_down[None], grad_up[None]


def solution(mesh):
    return jax.shard_map(
        body,
        mesh=mesh,
        in_specs=(
            P(("fsdp", "dp"), None),
            P(("fsdp", "dp"), None),
            P(),
            P(("fsdp", "dp"), None),
            P(),
            P("fsdp", None, None),
            P("fsdp", None, None),
            P(("fsdp", "dp"), None),
        ),
        out_specs=(P(("fsdp", "dp"), None), P("fsdp", "dp", None), P("fsdp", None, "dp")),
        check_vma=False,
    )
```

```python
import functools

import jax
import jax.numpy as jnp
from jax import lax
from jax.experimental import pallas as pl
from jax.experimental.pallas import tpu as pltpu
from jax.sharding import Mesh
from jax.sharding import PartitionSpec as P


SLOTS = 3
Q = 8
FSDP = ("x", "z", "yh")
DP = ("yl", "core")
PLANE = ("z", "yh", "yl")
F32 = jnp.float32
BF16 = jnp.bfloat16


def iota(shape, dimension):
    return lax.broadcasted_iota(jnp.int32, shape, dimension)


def nn(a, b):
    return lax.dot_general(a, b, (((1,), (0,)), ((), ())), preferred_element_type=F32)


def nt(a, b):
    return lax.dot_general(a, b, (((1,), (1,)), ((), ())), preferred_element_type=F32)


def tn(a, b):
    return lax.dot_general(a, b, (((0,), (0,)), ((), ())), preferred_element_type=F32)


def dispatch_kernel(storage_ref, index_ref, tokens_ref, cot_ref, sent_ref, place_ref, pick_ref):
    count, width = tokens_ref.shape
    rows = sent_ref.shape[0]
    chunk = width // Q
    half = cot_ref.shape[1] // 2
    index = index_ref[...]
    owner = jnp.zeros_like(index)
    for n in range(rows // Q):
        owner = jnp.where(index == n, storage_ref[n], owner)
    row = iota((rows, count), 0)
    q = row % Q
    mine = (row // Q) == jnp.broadcast_to(owner, (rows, count))
    mine_f = jnp.where(mine, 1.0, 0.0).astype(F32)
    earlier = jnp.where(iota((count, count), 0) < iota((count, count), 1), 1.0, 0.0).astype(BF16)
    rank = nn(mine_f.astype(BF16), earlier).astype(jnp.int32)
    for s in range(SLOTS):
        here = mine & (rank == s)
        for i in range(Q):
            pick_ref[s, :, i * count : (i + 1) * count] = jnp.where(
                here & (q == i), 1.0, 0.0
            ).astype(BF16)
    for h in range(2):
        both = mine & (rank == q // 2) & (q % 2 == h)
        place_ref[h] = jnp.where(both, 1.0, 0.0).astype(BF16)
        sent = nn(place_ref[h], cot_ref[:, h * half : (h + 1) * half])
        if h == 0:
            total = sent
        else:
            total = total + sent
    sent_ref[:, SLOTS * chunk :] = total.astype(BF16)
    step = 256

    @pl.loop(0, chunk // step)
    def _(block):
        start = block * step
        piece = jnp.concatenate(
            [
                tokens_ref[:, pl.ds(pl.multiple_of(i * chunk + start, step), step)]
                for i in range(Q)
            ],
            axis=0,
        )
        for s in range(SLOTS):
            sent_ref[:, pl.ds(pl.multiple_of(s * chunk + start, step), step)] = nn(
                pick_ref[s], piece
            ).astype(BF16)


def fold(masked, rank):
    rows, wide = masked.shape
    total = masked[:, : 2 * rank]
    for k in range(1, wide // (2 * rank)):
        total = total + masked[:, 2 * rank * k : 2 * rank * (k + 1)]
    total = total + pltpu.roll(total, rank, 1)
    total = jnp.sum(total.reshape(rows // Q, Q, 2 * rank), axis=1, keepdims=True)
    return jnp.broadcast_to(total, (rows // Q, Q, 2 * rank)).reshape(rows, 2 * rank)


def stacked_up(up_ref):
    half = up_ref.shape[1] // 2
    return jnp.concatenate([up_ref[:, :half], up_ref[:, half:]], axis=0)


def correct_kernel(arrived_ref, down_ref, up_ref, back_ref, low_ref):
    rows = arrived_ref.shape[0]
    rank, width = down_ref.shape
    chunk = width // Q
    q = iota((rows, 2 * rank), 0) % Q
    part = iota((rows, 2 * rank), 1) // rank
    wide_q = iota((rows, Q * rank), 0) % Q == iota((rows, Q * rank), 1) // rank
    down = jnp.concatenate([down_ref[:, i * chunk : (i + 1) * chunk] for i in range(Q)], axis=0)
    low = jnp.zeros((rows, 2 * rank), F32)
    for s in range(SLOTS):
        full = nt(arrived_ref[:, s * chunk : (s + 1) * chunk], down)
        low = jnp.where(q // 2 == s, fold(jnp.where(wide_q, full, 0.0), rank), low)
    low = jnp.where(part == q % 2, low, 0.0).astype(BF16)
    low_ref[...] = low
    back_ref[...] = nn(low, stacked_up(up_ref)).astype(BF16)


def grads_kernel(arrived_ref, up_ref, low_ref, grad_ref):
    rows = arrived_ref.shape[0]
    rank = up_ref.shape[0]
    chunk = grad_ref.shape[1] - 2 * rank
    cot = arrived_ref[:, SLOTS * chunk :]
    q = iota((rows, 2 * rank), 0) % Q
    part = iota((rows, 2 * rank), 1) // rank
    wide_q = iota((rows, Q * rank), 0) % Q == iota((rows, Q * rank), 1) // rank
    both = nt(cot, stacked_up(up_ref))
    lefts = []
    for s in range(SLOTS):
        back = fold(jnp.where((q // 2 == s) & (part == q % 2), both, 0.0), rank)
        lefts.append(
            jnp.where(wide_q, jnp.concatenate([back] * (Q // 2), axis=1), 0.0).astype(BF16)
        )
    left = jnp.concatenate(lefts, axis=0)
    step = 256
    for start in range(0, chunk, step):
        right = jnp.concatenate(
            [
                arrived_ref[:, s * chunk + start : s * chunk + start + step]
                for s in range(SLOTS)
            ],
            axis=0,
        )
        grad_ref[:, start : start + step] = tn(left, right).astype(BF16)
    up = tn(low_ref[...], cot).astype(BF16)
    per_half = Q // 2
    for d in range(Q):
        column = (d % per_half) // 2 * 2 * rank
        first = d // per_half * rank
        grad_ref[d * rank : (d + 1) * rank, chunk:] = up[
            first : first + rank, column : column + 2 * rank
        ]


def base_kernel(count_x, where_ref, tokens_ref, bias_ref, gate_ref, *refs):
    own, other, base_ref = refs[:count_x], refs[count_x : 2 * count_x], refs[-1]
    groups, block, out_width = own[0].shape
    depth = 2 * groups * block
    first = where_ref[1] == 0
    step = 16
    rows = 2 * step * block
    base_ref[...] = jnp.broadcast_to(bias_ref[...].astype(F32), base_ref.shape)
    for k in range(count_x):
        start = lax.rem(where_ref[0] + count_x - k, count_x) * depth

        @pl.loop(0, groups // step)
        def _(i):
            mine = own[k][pl.ds(i * step, step)]
            theirs = other[k][pl.ds(i * step, step)]
            low = jnp.where(first, mine, theirs)
            high = jnp.where(first, theirs, mine)
            weight = jnp.concatenate(
                [low.reshape(step, 1, block, out_width), high.reshape(step, 1, block, out_width)],
                axis=1,
            ).reshape(rows, out_width)
            columns = pl.ds(pl.multiple_of(start + i * rows, rows), rows)
            base_ref[...] += nn(tokens_ref[:, columns], weight)


def gate_kernel(*refs):
    refs[-1][...] = jnp.zeros_like(refs[-1])


def place_kernel(base_ref, place_ref, back_ref, values_ref):
    half = back_ref.shape[1]
    for h in range(2):
        placed = tn(place_ref[h], back_ref[...])
        columns = slice(h * half, (h + 1) * half)
        values_ref[:, columns] = (base_ref[:, columns] + placed).astype(BF16)


def vmem(number):
    return [pl.BlockSpec(memory_space=pltpu.VMEM)] * number


PARAMS = pltpu.CompilerParams(vmem_limit_bytes=48 << 20)


def body(
    tokens,
    token_adapter_index,
    adapter_storage_index,
    frozen_value_weight,
    frozen_value_bias,
    adapter_down_weight,
    adapter_up_weight,
    cotangent,
):
    count, width = tokens.shape
    out_width = frozen_value_weight.shape[1]
    fsdp = lax.axis_size(FSDP)
    dp = lax.axis_size(DP)
    size_x = lax.axis_size("x")
    rank = adapter_up_weight.shape[1]
    half = out_width // 2
    chunk = width // Q
    rows = fsdp * Q
    columns = SLOTS * chunk + half

    plane = lax.axis_size(PLANE)
    piece = lax.all_to_all(
        jnp.broadcast_to(frozen_value_weight[None], (plane, *frozen_value_weight.shape)),
        PLANE,
        split_axis=0,
        concat_axis=0,
        tiled=True,
    )
    sent, place = pl.pallas_call(
        dispatch_kernel,
        out_shape=(
            jax.ShapeDtypeStruct((rows, columns), BF16),
            jax.ShapeDtypeStruct((2, rows, count), BF16),
        ),
        in_specs=[pl.BlockSpec(memory_space=pltpu.SMEM)] + vmem(3),
        out_specs=tuple(vmem(2)),
        scratch_shapes=[pltpu.VMEM((SLOTS, rows, Q * count), BF16)],
        compiler_params=PARAMS,
        name="dispatch",
    )(adapter_storage_index, token_adapter_index.reshape(1, count), tokens, cotangent)
    sent, piece = lax.optimization_barrier((sent, piece))
    own = [piece]
    for k in range(1, size_x):
        shift = [(i, (i + k) % size_x) for i in range(size_x)]
        own.append(lax.ppermute(piece, "x", shift))
    other = []
    for k in range(size_x):
        other.append(lax.ppermute(own[k], "core", [(0, 1), (1, 0)]))
    gate = pl.pallas_call(
        gate_kernel,
        out_shape=jax.ShapeDtypeStruct((8, 128), F32),
        in_specs=[pl.BlockSpec(memory_space=pl.ANY)] * size_x,
        out_specs=vmem(1)[0],
        name="gate",
    )(*own[1:], other[0])
    arrived = lax.all_to_all(
        sent.reshape(fsdp, Q, columns), FSDP, split_axis=0, concat_axis=0, tiled=True
    ).reshape(rows, columns)
    down = jnp.swapaxes(adapter_down_weight[0], 0, 1)
    up = adapter_up_weight[0]
    back, low = pl.pallas_call(
        correct_kernel,
        out_shape=(
            jax.ShapeDtypeStruct((rows, half), BF16),
            jax.ShapeDtypeStruct((rows, 2 * rank), BF16),
        ),
        in_specs=vmem(3),
        out_specs=tuple(vmem(2)),
        compiler_params=PARAMS,
        name="correct",
    )(arrived, down, up)
    back = lax.all_to_all(
        back.reshape(fsdp, Q, half), FSDP, split_axis=0, concat_axis=0, tiled=True
    ).reshape(rows, half)
    grads = pl.pallas_call(
        grads_kernel,
        out_shape=jax.ShapeDtypeStruct((dp * rank, chunk + 2 * rank), BF16),
        in_specs=vmem(3),
        out_specs=vmem(1)[0],
        compiler_params=PARAMS,
        name="grads",
    )(arrived, up, low)
    grads = lax.all_to_all(
        grads.reshape(dp, rank, chunk + 2 * rank),
        DP,
        split_axis=0,
        concat_axis=0,
        tiled=True,
    )
    grads = jnp.sum(grads.astype(F32), axis=0)
    odd = lax.axis_index("core") == 1
    grad_up = jnp.where(odd, grads[:, chunk + rank :], grads[:, chunk : chunk + rank])
    grad_down = jnp.swapaxes(grads[:, :chunk], 0, 1)
    where = jnp.stack([lax.axis_index("x"), lax.axis_index("core")]).astype(jnp.int32)
    base = pl.pallas_call(
        functools.partial(base_kernel, size_x),
        out_shape=jax.ShapeDtypeStruct((count, out_width), F32),
        in_specs=[pl.BlockSpec(memory_space=pltpu.SMEM)] + vmem(3 + 2 * size_x),
        out_specs=vmem(1)[0],
        compiler_params=PARAMS,
        name="base",
    )(where, tokens, frozen_value_bias.reshape(1, out_width), gate, *own, *other)
    values = pl.pallas_call(
        place_kernel,
        out_shape=jax.ShapeDtypeStruct((count, out_width), BF16),
        in_specs=vmem(3),
        out_specs=vmem(1)[0],
        compiler_params=PARAMS,
        name="place",
    )(base, place, back)
    return values, grad_down[None], grad_up[None]


def solution(mesh):
    fine = Mesh(mesh.devices.reshape(4, 8, 2, 4, 2), FSDP + DP)
    all_axes = FSDP + DP
    return jax.shard_map(
        body,
        mesh=fine,
        in_specs=(
            P(all_axes, None),
            P(all_axes, None),
            P(),
            P(all_axes, None),
            P(),
            P(FSDP, None, None),
            P(FSDP, None, None),
            P(all_axes, None),
        ),
        out_specs=(P(all_axes, None), P(FSDP, DP, None), P(FSDP, None, DP)),
        check_vma=False,
    )
```

```python
import functools

import jax
import jax.numpy as jnp
from jax import lax
from jax.experimental import pallas as pl
from jax.experimental.pallas import tpu as pltpu
from jax.sharding import Mesh
from jax.sharding import PartitionSpec as P


SLOTS = 3
Q = 8
FSDP = ("x", "z", "yh")
DP = ("yl", "core")
COLUMN = ("yh", "yl")
SWAP = ((0, 1), (1, 0))
F32 = jnp.float32
BF16 = jnp.bfloat16


def iota(shape, dimension):
    return lax.broadcasted_iota(jnp.int32, shape, dimension)


def nn(a, b):
    return lax.dot_general(a, b, (((1,), (0,)), ((), ())), preferred_element_type=F32)


def nt(a, b):
    return lax.dot_general(a, b, (((1,), (1,)), ((), ())), preferred_element_type=F32)


def tn(a, b):
    return lax.dot_general(a, b, (((0,), (0,)), ((), ())), preferred_element_type=F32)


def dispatch_kernel(storage_ref, index_ref, tokens_ref, cot_ref, sent_ref, place_ref, pick_ref):
    count, width = tokens_ref.shape
    rows = sent_ref.shape[0]
    chunk = width // Q
    half = cot_ref.shape[1] // 2
    index = index_ref[...]
    owner = jnp.zeros_like(index)
    for n in range(rows // Q):
        owner = jnp.where(index == n, storage_ref[n], owner)
    row = iota((rows, count), 0)
    q = row % Q
    mine = (row // Q) == jnp.broadcast_to(owner, (rows, count))
    mine_f = jnp.where(mine, 1.0, 0.0).astype(F32)
    earlier = jnp.where(iota((count, count), 0) < iota((count, count), 1), 1.0, 0.0).astype(BF16)
    rank = nn(mine_f.astype(BF16), earlier).astype(jnp.int32)
    for s in range(SLOTS):
        here = mine & (rank == s)
        for i in range(Q):
            pick_ref[s, :, i * count : (i + 1) * count] = jnp.where(
                here & (q == i), 1.0, 0.0
            ).astype(BF16)
    for h in range(2):
        both = mine & (rank == q // 2) & (q % 2 == h)
        place_ref[h] = jnp.where(both, 1.0, 0.0).astype(BF16)
        sent = nn(place_ref[h], cot_ref[:, h * half : (h + 1) * half])
        if h == 0:
            total = sent
        else:
            total = total + sent
    sent_ref[:, SLOTS * chunk :] = total.astype(BF16)
    step = 256

    @pl.loop(0, chunk // step)
    def _(block):
        start = block * step
        piece = jnp.concatenate(
            [
                tokens_ref[:, pl.ds(pl.multiple_of(i * chunk + start, step), step)]
                for i in range(Q)
            ],
            axis=0,
        )
        for s in range(SLOTS):
            sent_ref[:, pl.ds(pl.multiple_of(s * chunk + start, step), step)] = nn(
                pick_ref[s], piece
            ).astype(BF16)


def fold(masked, rank):
    rows, wide = masked.shape
    total = masked[:, : 2 * rank]
    for k in range(1, wide // (2 * rank)):
        total = total + masked[:, 2 * rank * k : 2 * rank * (k + 1)]
    total = total + pltpu.roll(total, rank, 1)
    total = jnp.sum(total.reshape(rows // Q, Q, 2 * rank), axis=1, keepdims=True)
    return jnp.broadcast_to(total, (rows // Q, Q, 2 * rank)).reshape(rows, 2 * rank)


def stacked_up(up_ref):
    half = up_ref.shape[1] // 2
    return jnp.concatenate([up_ref[:, :half], up_ref[:, half:]], axis=0)


def correct_kernel(arrived_ref, down_ref, up_ref, back_ref, low_ref):
    rows = arrived_ref.shape[0]
    rank, width = down_ref.shape
    chunk = width // Q
    q = iota((rows, 2 * rank), 0) % Q
    part = iota((rows, 2 * rank), 1) // rank
    wide_q = iota((rows, Q * rank), 0) % Q == iota((rows, Q * rank), 1) // rank
    down = jnp.concatenate([down_ref[:, i * chunk : (i + 1) * chunk] for i in range(Q)], axis=0)
    low = jnp.zeros((rows, 2 * rank), F32)
    for s in range(SLOTS):
        full = nt(arrived_ref[:, s * chunk : (s + 1) * chunk], down)
        low = jnp.where(q // 2 == s, fold(jnp.where(wide_q, full, 0.0), rank), low)
    low = jnp.where(part == q % 2, low, 0.0).astype(BF16)
    low_ref[...] = low
    back_ref[...] = nn(low, stacked_up(up_ref)).astype(BF16)


def grads_kernel(where_ref, arrived_ref, up_ref, low_ref, keep_ref, give_ref, grad_ref):
    rows = arrived_ref.shape[0]
    rank = up_ref.shape[0]
    chunk = grad_ref.shape[1] - 2 * rank
    cot = arrived_ref[:, SLOTS * chunk :]
    q = iota((rows, 2 * rank), 0) % Q
    part = iota((rows, 2 * rank), 1) // rank
    wide_q = iota((rows, Q * rank), 0) % Q == iota((rows, Q * rank), 1) // rank
    both = nt(cot, stacked_up(up_ref))
    lefts = []
    for s in range(SLOTS):
        back = fold(jnp.where((q // 2 == s) & (part == q % 2), both, 0.0), rank)
        lefts.append(
            jnp.where(wide_q, jnp.concatenate([back] * (Q // 2), axis=1), 0.0).astype(BF16)
        )
    left = jnp.concatenate(lefts, axis=0)
    step = 256
    for start in range(0, chunk, step):
        right = jnp.concatenate(
            [
                arrived_ref[:, s * chunk + start : s * chunk + start + step]
                for s in range(SLOTS)
            ],
            axis=0,
        )
        grad_ref[:, start : start + step] = tn(left, right)
    up = tn(low_ref[...], cot)
    per_half = Q // 2
    for d in range(Q):
        column = (d % per_half) // 2 * 2 * rank
        first = d // per_half * rank
        grad_ref[d * rank : (d + 1) * rank, chunk:] = up[
            first : first + rank, column : column + 2 * rank
        ]
    core = where_ref[3]
    for y in range(Q // 2):
        block = slice(y * rank, (y + 1) * rank)
        keep_ref[block] = grad_ref[pl.ds(pl.multiple_of((2 * y + core) * rank, rank), rank)]
        give_ref[block] = grad_ref[
            pl.ds(pl.multiple_of((2 * y + 1 - core) * rank, rank), rank)
        ].astype(BF16)


def middle_kernel(where_ref, keep_ref, taken_ref, mine_ref, *sent_refs):
    count = 1 + len(sent_refs)
    rank = mine_ref.shape[0]
    for k in range(count):
        y = lax.rem(where_ref[2] + k, count)
        rows = pl.ds(pl.multiple_of(y * rank, rank), rank)
        total = keep_ref[rows] + taken_ref[rows].astype(F32)
        if k == 0:
            mine_ref[...] = total
        else:
            sent_refs[k - 1][...] = total.astype(BF16)


def finish_kernel(where_ref, mine_ref, *refs):
    taken, (down_ref, up_ref) = refs[:-2], refs[-2:]
    rank = mine_ref.shape[0]
    chunk = down_ref.shape[1]
    total = mine_ref[...]
    for ref in taken:
        total = total + ref[...].astype(F32)
    down_ref[...] = total[:, :chunk]
    up_ref[...] = jnp.where(
        where_ref[3] == 1, pltpu.roll(total[:, chunk:], rank, 1), total[:, chunk:]
    )[:, :rank]


def base_kernel(size_x, size_z, where_ref, tokens_ref, bias_ref, gate_ref, *refs):
    own, other, base_ref = refs[:size_x], refs[size_x : 2 * size_x], refs[-1]
    groups, block, out_width = own[0].shape
    step = groups // size_z
    rows = 2 * step * block
    first = where_ref[3] == 0
    base_ref[...] = jnp.broadcast_to(bias_ref[...].astype(F32), base_ref.shape)
    for k in range(size_x):
        from_x = lax.rem(where_ref[0] + size_x - k, size_x)

        @pl.loop(0, size_z)
        def _(i):
            from_z = lax.rem(where_ref[1] + size_z - i, size_z)
            mine = own[k][pl.ds(i * step, step)]
            theirs = other[k][pl.ds(i * step, step)]
            low = jnp.where(first, mine, theirs)
            high = jnp.where(first, theirs, mine)
            weight = jnp.concatenate(
                [low.reshape(step, 1, block, out_width), high.reshape(step, 1, block, out_width)],
                axis=1,
            ).reshape(rows, out_width)
            columns = pl.ds(pl.multiple_of((from_x * size_z + from_z) * rows, rows), rows)
            base_ref[...] += nn(tokens_ref[:, columns], weight)


def gate_kernel(*refs):
    refs[-1][...] = jnp.zeros_like(refs[-1])


def place_kernel(base_ref, place_ref, back_ref, values_ref):
    half = back_ref.shape[1]
    for h in range(2):
        placed = tn(place_ref[h], back_ref[...])
        columns = slice(h * half, (h + 1) * half)
        values_ref[:, columns] = (base_ref[:, columns] + placed).astype(BF16)


def vmem(number):
    return [pl.BlockSpec(memory_space=pltpu.VMEM)] * number


PARAMS = pltpu.CompilerParams(vmem_limit_bytes=48 << 20)


def body(
    tokens,
    token_adapter_index,
    adapter_storage_index,
    frozen_value_weight,
    frozen_value_bias,
    adapter_down_weight,
    adapter_up_weight,
    cotangent,
):
    count, width = tokens.shape
    out_width = frozen_value_weight.shape[1]
    fsdp = lax.axis_size(FSDP)
    dp = lax.axis_size(DP)
    size_x = lax.axis_size("x")
    size_z = lax.axis_size("z")
    size_y = lax.axis_size("yl")
    where = jnp.stack([lax.axis_index(n) for n in ("x", "z", "yl", "core")]).astype(jnp.int32)
    smem = [pl.BlockSpec(memory_space=pltpu.SMEM)]
    rank = adapter_up_weight.shape[1]
    half = out_width // 2
    chunk = width // Q
    rows = fsdp * Q
    columns = SLOTS * chunk + half

    column = lax.all_gather(frozen_value_weight, COLUMN, axis=0, tiled=True)
    sent, place = pl.pallas_call(
        dispatch_kernel,
        out_shape=(
            jax.ShapeDtypeStruct((rows, columns), BF16),
            jax.ShapeDtypeStruct((2, rows, count), BF16),
        ),
        in_specs=[pl.BlockSpec(memory_space=pltpu.SMEM)] + vmem(3),
        out_specs=tuple(vmem(2)),
        scratch_shapes=[pltpu.VMEM((SLOTS, rows, Q * count), BF16)],
        compiler_params=PARAMS,
        name="dispatch",
    )(adapter_storage_index, token_adapter_index.reshape(1, count), tokens, cotangent)
    sent, column = lax.optimization_barrier((sent, column))
    parts = [column]
    for k in range(1, size_z):
        climb = [(i, (i + k) % size_z) for i in range(size_z)]
        parts.append(lax.ppermute(column, "z", climb))
    piece = jnp.concatenate(parts, axis=0).reshape(-1, *frozen_value_weight.shape)
    own = [piece]
    for k in range(1, size_x):
        shift = [(i, (i + k) % size_x) for i in range(size_x)]
        own.append(lax.ppermute(piece, "x", shift))
    other = []
    for k in range(size_x):
        other.append(lax.ppermute(own[k], "core", SWAP))
    gate = pl.pallas_call(
        gate_kernel,
        out_shape=jax.ShapeDtypeStruct((8, 128), F32),
        in_specs=[pl.BlockSpec(memory_space=pl.ANY)],
        out_specs=vmem(1)[0],
        name="gate",
    )(other[0])
    arrived = lax.all_to_all(
        sent.reshape(fsdp, Q, columns), FSDP, split_axis=0, concat_axis=0, tiled=True
    ).reshape(rows, columns)
    down = jnp.swapaxes(adapter_down_weight[0], 0, 1)
    up = adapter_up_weight[0]
    back, low = pl.pallas_call(
        correct_kernel,
        out_shape=(
            jax.ShapeDtypeStruct((rows, half), BF16),
            jax.ShapeDtypeStruct((rows, 2 * rank), BF16),
        ),
        in_specs=vmem(3),
        out_specs=tuple(vmem(2)),
        compiler_params=PARAMS,
        name="correct",
    )(arrived, down, up)
    back = lax.all_to_all(
        back.reshape(fsdp, Q, half), FSDP, split_axis=0, concat_axis=0, tiled=True
    ).reshape(rows, half)
    wide = chunk + 2 * rank
    keep, give = pl.pallas_call(
        grads_kernel,
        out_shape=(
            jax.ShapeDtypeStruct((size_y * rank, wide), F32),
            jax.ShapeDtypeStruct((size_y * rank, wide), BF16),
        ),
        in_specs=smem + vmem(3),
        out_specs=tuple(vmem(2)),
        scratch_shapes=[pltpu.VMEM((dp * rank, wide), F32)],
        compiler_params=PARAMS,
        name="grads",
    )(where, arrived, up, low)
    taken = lax.ppermute(give, "core", SWAP)
    mine, *sums = pl.pallas_call(
        middle_kernel,
        out_shape=(jax.ShapeDtypeStruct((rank, wide), F32),)
        + (jax.ShapeDtypeStruct((rank, wide), BF16),) * (size_y - 1),
        in_specs=smem + vmem(2),
        out_specs=tuple(vmem(size_y)),
        compiler_params=PARAMS,
        name="middle",
    )(where, keep, taken)
    arrivals = []
    for k in range(1, size_y):
        rise = [(i, (i + k) % size_y) for i in range(size_y)]
        arrivals.append(lax.ppermute(sums[k - 1], "yl", rise))
    base = pl.pallas_call(
        functools.partial(base_kernel, size_x, size_z),
        out_shape=jax.ShapeDtypeStruct((count, out_width), F32),
        in_specs=smem + vmem(3 + 2 * size_x),
        out_specs=vmem(1)[0],
        compiler_params=PARAMS,
        name="base",
    )(where, tokens, frozen_value_bias.reshape(1, out_width), gate, *own, *other)
    values = pl.pallas_call(
        place_kernel,
        out_shape=jax.ShapeDtypeStruct((count, out_width), BF16),
        in_specs=vmem(3),
        out_specs=vmem(1)[0],
        compiler_params=PARAMS,
        name="place",
    )(base, place, back)
    grad_down, grad_up = pl.pallas_call(
        finish_kernel,
        out_shape=(
            jax.ShapeDtypeStruct((rank, chunk), F32),
            jax.ShapeDtypeStruct((rank, rank), F32),
        ),
        in_specs=smem + vmem(size_y),
        out_specs=tuple(vmem(2)),
        compiler_params=PARAMS,
        name="finish",
    )(where, mine, *arrivals)
    return values, jnp.swapaxes(grad_down, 0, 1)[None], grad_up[None]


def solution(mesh):
    fine = Mesh(mesh.devices.reshape(4, 8, 2, 4, 2), FSDP + DP)
    all_axes = FSDP + DP
    return jax.shard_map(
        body,
        mesh=fine,
        in_specs=(
            P(all_axes, None),
            P(all_axes, None),
            P(),
            P(all_axes, None),
            P(),
            P(FSDP, None, None),
            P(FSDP, None, None),
            P(all_axes, None),
        ),
        out_specs=(P(all_axes, None), P(FSDP, DP, None), P(FSDP, None, DP)),
        check_vma=False,
    )
```

```python
import functools

import jax
import jax.numpy as jnp
from jax import lax
from jax.experimental import pallas as pl
from jax.experimental.pallas import tpu as pltpu
from jax.sharding import Mesh
from jax.sharding import PartitionSpec as P


SLOTS = 3
Q = 8
FSDP = ("x", "z", "yh")
DP = ("yl", "core")
PLANE = ("z", "yh", "yl")
SWAP = ((0, 1), (1, 0))
F32 = jnp.float32
BF16 = jnp.bfloat16


def iota(shape, dimension):
    return lax.broadcasted_iota(jnp.int32, shape, dimension)


def nn(a, b):
    return lax.dot_general(a, b, (((1,), (0,)), ((), ())), preferred_element_type=F32)


def nt(a, b):
    return lax.dot_general(a, b, (((1,), (1,)), ((), ())), preferred_element_type=F32)


def tn(a, b):
    return lax.dot_general(a, b, (((0,), (0,)), ((), ())), preferred_element_type=F32)


def dispatch_kernel(storage_ref, index_ref, tokens_ref, cot_ref, sent_ref, place_ref, pick_ref):
    count, width = tokens_ref.shape
    rows = sent_ref.shape[0]
    chunk = width // Q
    half = cot_ref.shape[1] // 2
    index = index_ref[...]
    owner = jnp.zeros_like(index)
    for n in range(rows // Q):
        owner = jnp.where(index == n, storage_ref[n], owner)
    row = iota((rows, count), 0)
    q = row % Q
    mine = (row // Q) == jnp.broadcast_to(owner, (rows, count))
    mine_f = jnp.where(mine, 1.0, 0.0).astype(F32)
    earlier = jnp.where(iota((count, count), 0) < iota((count, count), 1), 1.0, 0.0).astype(BF16)
    rank = nn(mine_f.astype(BF16), earlier).astype(jnp.int32)
    for s in range(SLOTS):
        here = mine & (rank == s)
        for i in range(Q):
            pick_ref[s, :, i * count : (i + 1) * count] = jnp.where(
                here & (q == i), 1.0, 0.0
            ).astype(BF16)
    for h in range(2):
        both = mine & (rank == q // 2) & (q % 2 == h)
        place_ref[h] = jnp.where(both, 1.0, 0.0).astype(BF16)
        sent = nn(place_ref[h], cot_ref[:, h * half : (h + 1) * half])
        if h == 0:
            total = sent
        else:
            total = total + sent
    sent_ref[:, SLOTS * chunk :] = total.astype(BF16)
    step = 256

    @pl.loop(0, chunk // step)
    def _(block):
        start = block * step
        piece = jnp.concatenate(
            [
                tokens_ref[:, pl.ds(pl.multiple_of(i * chunk + start, step), step)]
                for i in range(Q)
            ],
            axis=0,
        )
        for s in range(SLOTS):
            sent_ref[:, pl.ds(pl.multiple_of(s * chunk + start, step), step)] = nn(
                pick_ref[s], piece
            ).astype(BF16)


def fold(masked, rank):
    rows, wide = masked.shape
    total = masked[:, : 2 * rank]
    for k in range(1, wide // (2 * rank)):
        total = total + masked[:, 2 * rank * k : 2 * rank * (k + 1)]
    total = total + pltpu.roll(total, rank, 1)
    total = jnp.sum(total.reshape(rows // Q, Q, 2 * rank), axis=1, keepdims=True)
    return jnp.broadcast_to(total, (rows // Q, Q, 2 * rank)).reshape(rows, 2 * rank)


def stacked_up(up_ref):
    half = up_ref.shape[1] // 2
    return jnp.concatenate([up_ref[:, :half], up_ref[:, half:]], axis=0)


def correct_kernel(arrived_ref, down_ref, up_ref, back_ref, low_ref):
    rows = arrived_ref.shape[0]
    rank, width = down_ref.shape
    chunk = width // Q
    q = iota((rows, 2 * rank), 0) % Q
    part = iota((rows, 2 * rank), 1) // rank
    wide_q = iota((rows, Q * rank), 0) % Q == iota((rows, Q * rank), 1) // rank
    down = jnp.concatenate([down_ref[:, i * chunk : (i + 1) * chunk] for i in range(Q)], axis=0)
    low = jnp.zeros((rows, 2 * rank), F32)
    for s in range(SLOTS):
        full = nt(arrived_ref[:, s * chunk : (s + 1) * chunk], down)
        low = jnp.where(q // 2 == s, fold(jnp.where(wide_q, full, 0.0), rank), low)
    low = jnp.where(part == q % 2, low, 0.0).astype(BF16)
    low_ref[...] = low
    back_ref[...] = nn(low, stacked_up(up_ref)).astype(BF16)


def grads_kernel(where_ref, arrived_ref, up_ref, low_ref, keep_ref, give_ref, grad_ref):
    rows = arrived_ref.shape[0]
    rank = up_ref.shape[0]
    chunk = grad_ref.shape[1] - 2 * rank
    cot = arrived_ref[:, SLOTS * chunk :]
    q = iota((rows, 2 * rank), 0) % Q
    part = iota((rows, 2 * rank), 1) // rank
    wide_q = iota((rows, Q * rank), 0) % Q == iota((rows, Q * rank), 1) // rank
    both = nt(cot, stacked_up(up_ref))
    lefts = []
    for s in range(SLOTS):
        back = fold(jnp.where((q // 2 == s) & (part == q % 2), both, 0.0), rank)
        lefts.append(
            jnp.where(wide_q, jnp.concatenate([back] * (Q // 2), axis=1), 0.0).astype(BF16)
        )
    left = jnp.concatenate(lefts, axis=0)
    step = 256
    for start in range(0, chunk, step):
        right = jnp.concatenate(
            [
                arrived_ref[:, s * chunk + start : s * chunk + start + step]
                for s in range(SLOTS)
            ],
            axis=0,
        )
        grad_ref[:, start : start + step] = tn(left, right)
    up = tn(low_ref[...], cot)
    per_half = Q // 2
    for d in range(Q):
        column = (d % per_half) // 2 * 2 * rank
        first = d // per_half * rank
        grad_ref[d * rank : (d + 1) * rank, chunk:] = up[
            first : first + rank, column : column + 2 * rank
        ]
    core = where_ref[3]
    for y in range(Q // 2):
        block = slice(y * rank, (y + 1) * rank)
        keep_ref[block] = grad_ref[pl.ds(pl.multiple_of((2 * y + core) * rank, rank), rank)]
        give_ref[block] = grad_ref[
            pl.ds(pl.multiple_of((2 * y + 1 - core) * rank, rank), rank)
        ].astype(BF16)


def middle_kernel(where_ref, keep_ref, taken_ref, mine_ref, *sent_refs):
    count = 1 + len(sent_refs)
    rank = mine_ref.shape[0]
    for k in range(count):
        y = lax.rem(where_ref[2] + k, count)
        rows = pl.ds(pl.multiple_of(y * rank, rank), rank)
        total = keep_ref[rows] + taken_ref[rows].astype(F32)
        if k == 0:
            mine_ref[...] = total
        else:
            sent_refs[k - 1][...] = total.astype(BF16)


def finish_kernel(where_ref, mine_ref, *refs):
    taken, (down_ref, up_ref) = refs[:-2], refs[-2:]
    rank = mine_ref.shape[0]
    chunk = down_ref.shape[1]
    total = mine_ref[...]
    for ref in taken:
        total = total + ref[...].astype(F32)
    down_ref[...] = total[:, :chunk]
    up_ref[...] = jnp.where(
        where_ref[3] == 1, pltpu.roll(total[:, chunk:], rank, 1), total[:, chunk:]
    )[:, :rank]


def base_kernel(size_x, size_z, where_ref, tokens_ref, bias_ref, *refs):
    own, other, base_ref = refs[:size_x], refs[size_x : 2 * size_x], refs[-1]
    groups, block, out_width = own[0].shape
    step = groups // size_z
    rows = 2 * step * block
    first = where_ref[3] == 0
    base_ref[...] = jnp.broadcast_to(bias_ref[...].astype(F32), base_ref.shape)
    for k in range(size_x):
        from_x = lax.rem(where_ref[0] + size_x - k, size_x)

        @pl.loop(0, size_z)
        def _(i):
            mine = own[k][pl.ds(i * step, step)]
            theirs = other[k][pl.ds(i * step, step)]
            low = jnp.where(first, mine, theirs)
            high = jnp.where(first, theirs, mine)
            weight = jnp.concatenate(
                [low.reshape(step, 1, block, out_width), high.reshape(step, 1, block, out_width)],
                axis=1,
            ).reshape(rows, out_width)
            columns = pl.ds(pl.multiple_of((from_x * size_z + i) * rows, rows), rows)
            base_ref[...] += nn(tokens_ref[:, columns], weight)


def place_kernel(base_ref, place_ref, back_ref, values_ref):
    half = back_ref.shape[1]
    for h in range(2):
        placed = tn(place_ref[h], back_ref[...])
        columns = slice(h * half, (h + 1) * half)
        values_ref[:, columns] = (base_ref[:, columns] + placed).astype(BF16)


def vmem(number):
    return [pl.BlockSpec(memory_space=pltpu.VMEM)] * number


PARAMS = pltpu.CompilerParams(vmem_limit_bytes=48 << 20)


def body(
    tokens,
    token_adapter_index,
    adapter_storage_index,
    frozen_value_weight,
    frozen_value_bias,
    adapter_down_weight,
    adapter_up_weight,
    cotangent,
):
    count, width = tokens.shape
    out_width = frozen_value_weight.shape[1]
    fsdp = lax.axis_size(FSDP)
    dp = lax.axis_size(DP)
    size_x = lax.axis_size("x")
    size_z = lax.axis_size("z")
    size_y = lax.axis_size("yl")
    where = jnp.stack([lax.axis_index(n) for n in ("x", "z", "yl", "core")]).astype(jnp.int32)
    smem = [pl.BlockSpec(memory_space=pltpu.SMEM)]
    rank = adapter_up_weight.shape[1]
    half = out_width // 2
    chunk = width // Q
    rows = fsdp * Q
    columns = SLOTS * chunk + half

    plane = lax.axis_size(PLANE)
    piece = lax.all_to_all(
        jnp.broadcast_to(frozen_value_weight[None], (plane, *frozen_value_weight.shape)),
        PLANE,
        split_axis=0,
        concat_axis=0,
        tiled=True,
    )
    sent, place = pl.pallas_call(
        dispatch_kernel,
        out_shape=(
            jax.ShapeDtypeStruct((rows, columns), BF16),
            jax.ShapeDtypeStruct((2, rows, count), BF16),
        ),
        in_specs=[pl.BlockSpec(memory_space=pltpu.SMEM)] + vmem(3),
        out_specs=tuple(vmem(2)),
        scratch_shapes=[pltpu.VMEM((SLOTS, rows, Q * count), BF16)],
        compiler_params=PARAMS,
        name="dispatch",
    )(adapter_storage_index, token_adapter_index.reshape(1, count), tokens, cotangent)
    sent, piece = lax.optimization_barrier((sent, piece))
    own = [piece]
    for k in range(1, size_x):
        shift = [(i, (i + k) % size_x) for i in range(size_x)]
        own.append(lax.ppermute(piece, "x", shift))
    other = []
    for k in range(size_x):
        other.append(lax.ppermute(own[k], "core", SWAP))
    arrived = lax.all_to_all(
        sent.reshape(fsdp, Q, columns), FSDP, split_axis=0, concat_axis=0, tiled=True
    ).reshape(rows, columns)
    down = jnp.swapaxes(adapter_down_weight[0], 0, 1)
    up = adapter_up_weight[0]
    back, low = pl.pallas_call(
        correct_kernel,
        out_shape=(
            jax.ShapeDtypeStruct((rows, half), BF16),
            jax.ShapeDtypeStruct((rows, 2 * rank), BF16),
        ),
        in_specs=vmem(3),
        out_specs=tuple(vmem(2)),
        compiler_params=PARAMS,
        name="correct",
    )(arrived, down, up)
    back = lax.all_to_all(
        back.reshape(fsdp, Q, half), FSDP, split_axis=0, concat_axis=0, tiled=True
    ).reshape(rows, half)
    wide = chunk + 2 * rank
    keep, give = pl.pallas_call(
        grads_kernel,
        out_shape=(
            jax.ShapeDtypeStruct((size_y * rank, wide), F32),
            jax.ShapeDtypeStruct((size_y * rank, wide), BF16),
        ),
        in_specs=smem + vmem(3),
        out_specs=tuple(vmem(2)),
        scratch_shapes=[pltpu.VMEM((dp * rank, wide), F32)],
        compiler_params=PARAMS,
        name="grads",
    )(where, arrived, up, low)
    taken = lax.ppermute(give, "core", SWAP)
    mine, *sums = pl.pallas_call(
        middle_kernel,
        out_shape=(jax.ShapeDtypeStruct((rank, wide), F32),)
        + (jax.ShapeDtypeStruct((rank, wide), BF16),) * (size_y - 1),
        in_specs=smem + vmem(2),
        out_specs=tuple(vmem(size_y)),
        compiler_params=PARAMS,
        name="middle",
    )(where, keep, taken)
    arrivals = []
    for k in range(1, size_y):
        rise = [(i, (i + k) % size_y) for i in range(size_y)]
        arrivals.append(lax.ppermute(sums[k - 1], "yl", rise))
    base = pl.pallas_call(
        functools.partial(base_kernel, size_x, size_z),
        out_shape=jax.ShapeDtypeStruct((count, out_width), F32),
        in_specs=smem + vmem(2 + 2 * size_x),
        out_specs=vmem(1)[0],
        compiler_params=PARAMS,
        name="base",
    )(where, tokens, frozen_value_bias.reshape(1, out_width), *own, *other)
    values = pl.pallas_call(
        place_kernel,
        out_shape=jax.ShapeDtypeStruct((count, out_width), BF16),
        in_specs=vmem(3),
        out_specs=vmem(1)[0],
        compiler_params=PARAMS,
        name="place",
    )(base, place, back)
    grad_down, grad_up = pl.pallas_call(
        finish_kernel,
        out_shape=(
            jax.ShapeDtypeStruct((rank, chunk), F32),
            jax.ShapeDtypeStruct((rank, rank), F32),
        ),
        in_specs=smem + vmem(size_y),
        out_specs=tuple(vmem(2)),
        compiler_params=PARAMS,
        name="finish",
    )(where, mine, *arrivals)
    return values, jnp.swapaxes(grad_down, 0, 1)[None], grad_up[None]


def solution(mesh):
    fine = Mesh(mesh.devices.reshape(4, 8, 2, 4, 2), FSDP + DP)
    all_axes = FSDP + DP
    return jax.shard_map(
        body,
        mesh=fine,
        in_specs=(
            P(all_axes, None),
            P(all_axes, None),
            P(),
            P(all_axes, None),
            P(),
            P(FSDP, None, None),
            P(FSDP, None, None),
            P(all_axes, None),
        ),
        out_specs=(P(all_axes, None), P(FSDP, DP, None), P(FSDP, None, DP)),
        check_vma=False,
    )
```

```python
import functools

import jax
import jax.numpy as jnp
from jax import lax
from jax.experimental import pallas as pl
from jax.experimental.pallas import tpu as pltpu
from jax.sharding import Mesh
from jax.sharding import PartitionSpec as P


SLOTS = 3
Q = 8
FSDP = ("x", "z", "yh")
DP = ("yl", "core")
PLANE = ("z", "yh", "yl")
SWAP = ((0, 1), (1, 0))
F32 = jnp.float32
BF16 = jnp.bfloat16


def iota(shape, dimension):
    return lax.broadcasted_iota(jnp.int32, shape, dimension)


def nn(a, b):
    return lax.dot_general(a, b, (((1,), (0,)), ((), ())), preferred_element_type=F32)


def nt(a, b):
    return lax.dot_general(a, b, (((1,), (1,)), ((), ())), preferred_element_type=F32)


def tn(a, b):
    return lax.dot_general(a, b, (((0,), (0,)), ((), ())), preferred_element_type=F32)


def dispatch_kernel(storage_ref, index_ref, tokens_ref, cot_ref, sent_ref, place_ref, pick_ref):
    count, width = tokens_ref.shape
    rows = sent_ref.shape[0]
    chunk = width // Q
    half = cot_ref.shape[1] // 2
    index = index_ref[...]
    owner = jnp.zeros_like(index)
    for n in range(rows // Q):
        owner = jnp.where(index == n, storage_ref[n], owner)
    row = iota((rows, count), 0)
    q = row % Q
    mine = (row // Q) == jnp.broadcast_to(owner, (rows, count))
    mine_f = jnp.where(mine, 1.0, 0.0).astype(F32)
    earlier = jnp.where(iota((count, count), 0) < iota((count, count), 1), 1.0, 0.0).astype(BF16)
    rank = nn(mine_f.astype(BF16), earlier).astype(jnp.int32)
    for s in range(SLOTS):
        here = mine & (rank == s)
        for i in range(Q):
            pick_ref[s, :, i * count : (i + 1) * count] = jnp.where(
                here & (q == i), 1.0, 0.0
            ).astype(BF16)
    for h in range(2):
        both = mine & (rank == q // 2) & (q % 2 == h)
        place_ref[h] = jnp.where(both, 1.0, 0.0).astype(BF16)
        sent = nn(place_ref[h], cot_ref[:, h * half : (h + 1) * half])
        if h == 0:
            total = sent
        else:
            total = total + sent
    sent_ref[:, SLOTS * chunk :] = total.astype(BF16)
    step = 256

    @pl.loop(0, chunk // step)
    def _(block):
        start = block * step
        piece = jnp.concatenate(
            [
                tokens_ref[:, pl.ds(pl.multiple_of(i * chunk + start, step), step)]
                for i in range(Q)
            ],
            axis=0,
        )
        for s in range(SLOTS):
            sent_ref[:, pl.ds(pl.multiple_of(s * chunk + start, step), step)] = nn(
                pick_ref[s], piece
            ).astype(BF16)


def fold(masked, rank):
    rows, wide = masked.shape
    total = masked[:, : 2 * rank]
    for k in range(1, wide // (2 * rank)):
        total = total + masked[:, 2 * rank * k : 2 * rank * (k + 1)]
    total = total + pltpu.roll(total, rank, 1)
    total = jnp.sum(total.reshape(rows // Q, Q, 2 * rank), axis=1, keepdims=True)
    return jnp.broadcast_to(total, (rows // Q, Q, 2 * rank)).reshape(rows, 2 * rank)


def stacked_up(up_ref):
    half = up_ref.shape[1] // 2
    return jnp.concatenate([up_ref[:, :half], up_ref[:, half:]], axis=0)


def correct_kernel(arrived_ref, down_ref, up_ref, back_ref, low_ref):
    rows = arrived_ref.shape[0]
    rank, width = down_ref.shape
    chunk = width // Q
    q = iota((rows, 2 * rank), 0) % Q
    part = iota((rows, 2 * rank), 1) // rank
    wide_q = iota((rows, Q * rank), 0) % Q == iota((rows, Q * rank), 1) // rank
    down = jnp.concatenate([down_ref[:, i * chunk : (i + 1) * chunk] for i in range(Q)], axis=0)
    low = jnp.zeros((rows, 2 * rank), F32)
    for s in range(SLOTS):
        full = nt(arrived_ref[:, s * chunk : (s + 1) * chunk], down)
        low = jnp.where(q // 2 == s, fold(jnp.where(wide_q, full, 0.0), rank), low)
    low = jnp.where(part == q % 2, low, 0.0).astype(BF16)
    low_ref[...] = low
    back_ref[...] = nn(low, stacked_up(up_ref)).astype(BF16)


def grads_kernel(where_ref, arrived_ref, up_ref, low_ref, keep_ref, give_ref):
    rows = arrived_ref.shape[0]
    rank = up_ref.shape[0]
    chunk = keep_ref.shape[1] - 2 * rank
    first = where_ref[3] == 0
    cot = arrived_ref[:, SLOTS * chunk :]
    q = iota((rows, 2 * rank), 0) % Q
    part = iota((rows, 2 * rank), 1) // rank
    wide_q = iota((rows, Q * rank), 0) % Q == iota((rows, Q * rank), 1) // rank
    both = nt(cot, stacked_up(up_ref))
    lefts = []
    for s in range(SLOTS):
        back = fold(jnp.where((q // 2 == s) & (part == q % 2), both, 0.0), rank)
        lefts.append(
            jnp.where(wide_q, jnp.concatenate([back] * (Q // 2), axis=1), 0.0).astype(BF16)
        )
    left = jnp.concatenate(lefts, axis=0)
    step = 256

    def put(low, high, y, columns):
        block = slice(y * rank, (y + 1) * rank)
        keep_ref[block, columns] = jnp.where(first, low, high)
        give_ref[block, columns] = jnp.where(first, high, low).astype(BF16)

    for start in range(0, chunk, step):
        right = jnp.concatenate(
            [
                arrived_ref[:, s * chunk + start : s * chunk + start + step]
                for s in range(SLOTS)
            ],
            axis=0,
        )
        both = tn(left, right).reshape(Q // 2, 2, rank, step)
        for y in range(Q // 2):
            put(both[y, 0], both[y, 1], y, slice(start, start + step))
    up = tn(low_ref[...], cot)
    per_half = Q // 2
    for y in range(Q // 2):
        d = 2 * y
        column = d % per_half * rank
        row = d // per_half * rank
        part = up[row : row + rank, column : column + 2 * rank]
        put(part, part, y, slice(chunk, chunk + 2 * rank))


def middle_kernel(where_ref, keep_ref, taken_ref, mine_ref, *sent_refs):
    count = 1 + len(sent_refs)
    rank = mine_ref.shape[0]
    for k in range(count):
        y = lax.rem(where_ref[2] + k, count)
        rows = pl.ds(pl.multiple_of(y * rank, rank), rank)
        total = keep_ref[rows] + taken_ref[rows].astype(F32)
        if k == 0:
            mine_ref[...] = total
        else:
            sent_refs[k - 1][...] = total.astype(BF16)


def finish_kernel(where_ref, mine_ref, *refs):
    taken, (down_ref, up_ref) = refs[:-2], refs[-2:]
    rank = mine_ref.shape[0]
    chunk = down_ref.shape[1]
    total = mine_ref[...]
    for ref in taken:
        total = total + ref[...].astype(F32)
    down_ref[...] = total[:, :chunk]
    up_ref[...] = jnp.where(
        where_ref[3] == 1, pltpu.roll(total[:, chunk:], rank, 1), total[:, chunk:]
    )[:, :rank]


def base_kernel(size_x, size_z, where_ref, tokens_ref, bias_ref, *refs):
    own, other, base_ref = refs[:size_x], refs[size_x : 2 * size_x], refs[-1]
    groups, block, out_width = own[0].shape
    step = groups // size_z
    rows = 2 * step * block
    first = where_ref[3] == 0
    base_ref[...] = jnp.broadcast_to(bias_ref[...].astype(F32), base_ref.shape)
    for k in range(size_x):
        from_x = lax.rem(where_ref[0] + size_x - k, size_x)

        @pl.loop(0, size_z)
        def _(i):
            mine = own[k][pl.ds(i * step, step)]
            theirs = other[k][pl.ds(i * step, step)]
            low = jnp.where(first, mine, theirs)
            high = jnp.where(first, theirs, mine)
            weight = jnp.concatenate(
                [low.reshape(step, 1, block, out_width), high.reshape(step, 1, block, out_width)],
                axis=1,
            ).reshape(rows, out_width)
            columns = pl.ds(pl.multiple_of((from_x * size_z + i) * rows, rows), rows)
            base_ref[...] += nn(tokens_ref[:, columns], weight)


def place_kernel(base_ref, place_ref, back_ref, values_ref):
    half = back_ref.shape[1]
    for h in range(2):
        placed = tn(place_ref[h], back_ref[...])
        columns = slice(h * half, (h + 1) * half)
        values_ref[:, columns] = (base_ref[:, columns] + placed).astype(BF16)


def spread_kernel(weight_ref, spread_ref, held_ref, sem):
    held_ref[...] = jnp.broadcast_to(weight_ref[...][None], held_ref.shape)
    copy = pltpu.make_async_copy(held_ref, spread_ref, sem)
    copy.start()
    copy.wait()


def vmem(number):
    return [pl.BlockSpec(memory_space=pltpu.VMEM)] * number


ANY = pl.BlockSpec(memory_space=pl.ANY)
PARAMS = pltpu.CompilerParams(vmem_limit_bytes=24 << 20)


def body(
    tokens,
    token_adapter_index,
    adapter_storage_index,
    frozen_value_weight,
    frozen_value_bias,
    adapter_down_weight,
    adapter_up_weight,
    cotangent,
):
    count, width = tokens.shape
    out_width = frozen_value_weight.shape[1]
    fsdp = lax.axis_size(FSDP)
    size_x = lax.axis_size("x")
    size_z = lax.axis_size("z")
    size_y = lax.axis_size("yl")
    where = jnp.stack([lax.axis_index(n) for n in ("x", "z", "yl", "core")]).astype(jnp.int32)
    smem = [pl.BlockSpec(memory_space=pltpu.SMEM)]
    rank = adapter_up_weight.shape[1]
    half = out_width // 2
    chunk = width // Q
    rows = fsdp * Q
    columns = SLOTS * chunk + half

    plane = lax.axis_size(PLANE)
    spread = (plane, *frozen_value_weight.shape)
    piece = lax.all_to_all(
        pl.pallas_call(
            spread_kernel,
            out_shape=jax.ShapeDtypeStruct(spread, BF16),
            in_specs=vmem(1),
            out_specs=ANY,
            scratch_shapes=[pltpu.VMEM(spread, BF16), pltpu.SemaphoreType.DMA],
            compiler_params=PARAMS,
            name="spread",
        )(frozen_value_weight),
        PLANE,
        split_axis=0,
        concat_axis=0,
        tiled=True,
    )
    sent, place = pl.pallas_call(
        dispatch_kernel,
        out_shape=(
            jax.ShapeDtypeStruct((rows, columns), BF16),
            jax.ShapeDtypeStruct((2, rows, count), BF16),
        ),
        in_specs=[pl.BlockSpec(memory_space=pltpu.SMEM)] + vmem(3),
        out_specs=tuple(vmem(2)),
        scratch_shapes=[pltpu.VMEM((SLOTS, rows, Q * count), BF16)],
        compiler_params=PARAMS,
        name="dispatch",
    )(adapter_storage_index, token_adapter_index.reshape(1, count), tokens, cotangent)
    sent, piece = lax.optimization_barrier((sent, piece))
    own = [piece]
    for k in range(1, size_x):
        shift = [(i, (i + k) % size_x) for i in range(size_x)]
        own.append(lax.ppermute(piece, "x", shift))
    other = []
    for k in range(size_x):
        other.append(lax.ppermute(own[k], "core", SWAP))
    arrived = lax.all_to_all(
        sent.reshape(fsdp, Q, columns), FSDP, split_axis=0, concat_axis=0, tiled=True
    ).reshape(rows, columns)
    down = jnp.swapaxes(adapter_down_weight[0], 0, 1)
    up = adapter_up_weight[0]
    back, low = pl.pallas_call(
        correct_kernel,
        out_shape=(
            jax.ShapeDtypeStruct((rows, half), BF16),
            jax.ShapeDtypeStruct((rows, 2 * rank), BF16),
        ),
        in_specs=vmem(3),
        out_specs=tuple(vmem(2)),
        compiler_params=PARAMS,
        name="correct",
    )(arrived, down, up)
    back = lax.all_to_all(
        back.reshape(fsdp, Q, half), FSDP, split_axis=0, concat_axis=0, tiled=True
    ).reshape(rows, half)
    wide = chunk + 2 * rank
    keep, give = pl.pallas_call(
        grads_kernel,
        out_shape=(
            jax.ShapeDtypeStruct((size_y * rank, wide), F32),
            jax.ShapeDtypeStruct((size_y * rank, wide), BF16),
        ),
        in_specs=smem + vmem(3),
        out_specs=tuple(vmem(2)),
        compiler_params=PARAMS,
        name="grads",
    )(where, arrived, up, low)
    taken = lax.ppermute(give, "core", SWAP)
    mine, *sums = pl.pallas_call(
        middle_kernel,
        out_shape=(jax.ShapeDtypeStruct((rank, wide), F32),)
        + (jax.ShapeDtypeStruct((rank, wide), BF16),) * (size_y - 1),
        in_specs=smem + vmem(2),
        out_specs=tuple(vmem(size_y)),
        compiler_params=PARAMS,
        name="middle",
    )(where, keep, taken)
    arrivals = []
    for k in range(1, size_y):
        rise = [(i, (i + k) % size_y) for i in range(size_y)]
        arrivals.append(lax.ppermute(sums[k - 1], "yl", rise))
    base = pl.pallas_call(
        functools.partial(base_kernel, size_x, size_z),
        out_shape=jax.ShapeDtypeStruct((count, out_width), F32),
        in_specs=smem + vmem(2 + 2 * size_x),
        out_specs=vmem(1)[0],
        compiler_params=PARAMS,
        name="base",
    )(where, tokens, frozen_value_bias.reshape(1, out_width), *own, *other)
    values = pl.pallas_call(
        place_kernel,
        out_shape=jax.ShapeDtypeStruct((count, out_width), BF16),
        in_specs=vmem(3),
        out_specs=vmem(1)[0],
        compiler_params=PARAMS,
        name="place",
    )(base, place, back)
    grad_down, grad_up = pl.pallas_call(
        finish_kernel,
        out_shape=(
            jax.ShapeDtypeStruct((rank, chunk), F32),
            jax.ShapeDtypeStruct((rank, rank), F32),
        ),
        in_specs=smem + vmem(size_y),
        out_specs=tuple(vmem(2)),
        compiler_params=PARAMS,
        name="finish",
    )(where, mine, *arrivals)
    return values, jnp.swapaxes(grad_down, 0, 1)[None], grad_up[None]


def solution(mesh):
    fine = Mesh(mesh.devices.reshape(4, 8, 2, 4, 2), FSDP + DP)
    all_axes = FSDP + DP
    return jax.shard_map(
        body,
        mesh=fine,
        in_specs=(
            P(all_axes, None),
            P(all_axes, None),
            P(),
            P(all_axes, None),
            P(),
            P(FSDP, None, None),
            P(FSDP, None, None),
            P(all_axes, None),
        ),
        out_specs=(P(all_axes, None), P(FSDP, DP, None), P(FSDP, None, DP)),
        check_vma=False,
    )
```
